32 devices in a mesh: cuts: 2 (over y), idx: 8 (over z, x), half: 2 (over core).
Axes of the slice: x: 2, y: 2, z: 4, core: 2. Of those that a mesh axis runs over, the one named last changes fastest.
Arguments:
- left_factor: float32 [2, 4, 64, 1024, 256], P('half', 'cuts', 'idx'), parts along dimension 1, may hold values from -6 to 6
- right_factor: float32 [2, 4, 64, 256, 1024], P('half', 'cuts', None, 'idx'), parts along dimension 1, may hold values from -0.25 to 0.25
Outputs:
- amplitudes: float32 [1024, 4, 1024], P(('idx', 'half'), 'cuts'), parts along dimension 1
The draws below stay inside these ranges and needn't reach their ends.
There are 2 independent parts, one for each index of `cuts`. The reference program is written for one: setup_inputs(seed, part) draws one part's arguments, and reference() takes and returns one part's arrays. A program takes and returns all parts, laid end to end along the dimension named above; each array names one. Nothing has to cross between parts.
All inputs are finite; a program needn't handle non-finite values.
Results may differ from the reference program's by a relative error of at most 0.0003.
Values sent between devices are 32-bit elements; how exact they have to be, the bound alone decides.
A program may use at most 256 MiB of HBM per device.

```python
import math
import jax
import jax.numpy as jnp
from jax import lax

BATCH = 64
M = 1024
K = 256
N = 1024


def strengthened(result, rng, source, target, shards_of, factor):
    def block_of(position):
        return (jnp.arange(result.shape[position]) // (result.shape[position] // shards_of)).reshape((-1,) + (1,) * (result.ndim - 1 - position))

    near = jax.random.permutation(rng, shards_of)[block_of(target)]
    far = (block_of(target) + shards_of // 2) % shards_of
    return jnp.where((block_of(source) == near) | (block_of(source) == far), factor * result, result)


def level_of(stream_key, extent, shards, smallest, top_value):
    def one(axis_at, blocks):
        draws = jax.random.uniform(jax.random.fold_in(jax.random.fold_in(stream_key, 6), axis_at), (blocks,), jnp.float32, smallest / len(shards), top_value / len(shards))
        return jnp.repeat(jnp.exp(draws), extent[axis_at] // blocks).reshape((-1,) + (1,) * (len(extent) - axis_at - 1))

    loudness = one(*shards[0])
    for cut in shards[1:]:
        loudness = loudness * one(*cut)
    return loudness


def centred(stream_key, shape, width, limit, pieces=(), held_as=jnp.bfloat16):
    entries = width * jax.random.normal(stream_key, shape, jnp.float32)
    if pieces:
        entries = entries * level_of(stream_key, shape, pieces, -0.22, 0.18)
    return jnp.clip(entries, -limit, limit).astype(held_as)


def heavy_noise(key, shape, spread, limit, shards, heavy, kind=jnp.bfloat16):
    values = spread * jax.random.normal(key, shape, jnp.float32)
    if shards:
        values = values * level_of(key, shape, shards, -0.22, 0.18)
    return jnp.clip(strengthened(values, jax.random.fold_in(key, 3), *heavy), -limit, limit).astype(kind)


def setup_inputs(seed: int = 0, part: int = 0) -> dict:
    splits = jax.random.split(jax.random.key(seed), 3)
    part_keys = jax.random.split(jax.random.fold_in(splits[2], part), 3)
    left_factor = heavy_noise(part_keys[0], (2, 2, BATCH, M, K), 1.0, 6.0, ((0, 2), (2, 8)), (2, 3, 8, 2.0), jnp.float32)
    right_factor = centred(part_keys[1], (2, 2, BATCH, K, N), (2 * K) ** -0.5, 0.25, ((0, 2), (3, 8)), jnp.float32)
    return dict(left_factor=left_factor, right_factor=right_factor)


def complex_product(left_real, left_imag, right_real, right_imag, pattern):
    highest = lax.Precision.HIGHEST
    real_part = jnp.einsum(pattern, left_real, right_real, precision=highest) - jnp.einsum(pattern, left_imag, right_imag, precision=highest)
    imag_part = jnp.einsum(pattern, left_real, right_imag, precision=highest) + jnp.einsum(pattern, left_imag, right_real, precision=highest)
    return (real_part, imag_part)

def reference(left_factor, right_factor):
    block_size = math.gcd(BATCH, 8)
    norm_scale = 1.0 / math.sqrt(2.0 * BATCH * N)

    def batch_block(running, block_index):
        first_row = (block_index * block_size).astype(jnp.int32)
        left_block = lax.dynamic_slice_in_dim(left_factor, first_row, block_size, 2)
        right_block = lax.dynamic_slice_in_dim(right_factor, first_row, block_size, 2)
        merged_zero = complex_product(left_block[0, 0], left_block[0, 1], right_block[0, 0], right_block[0, 1], 'bmk,bkn->bmn')
        merged_one = complex_product(left_block[1, 0], left_block[1, 1], right_block[1, 0], right_block[1, 1], 'bmk,bkn->bmn')
        real_part, imag_part = complex_product(merged_zero[0], merged_zero[1], merged_one[0], merged_one[1], 'bmn,bon->mo')
        return (running + jnp.stack([real_part, imag_part], axis=1) * norm_scale, None)
    start_value = jnp.zeros((M, 2, M), jnp.float32)
    total, unused = lax.scan(batch_block, start_value, jnp.arange(BATCH // block_size, dtype=jnp.int32))
    return total
```

```python
import math

import jax
import jax.numpy as jnp
from jax import lax
from jax.sharding import PartitionSpec as P

HIGH = lax.Precision.HIGH
CHUNKS = (3, 1)


def swapped(x, axis, bit):
    return lax.ppermute(x, axis, [(i, i ^ 1 << bit) for i in range(lax.axis_size(axis))])


def complex_product(left_real, left_imag, right_real, right_imag, pattern):
    first_term = jnp.einsum(pattern, left_real, right_real, precision=HIGH)
    second_term = jnp.einsum(pattern, left_imag, right_imag, precision=HIGH)
    mixed_term = jnp.einsum(
        pattern, left_real + left_imag, right_real + right_imag, precision=HIGH
    )
    return (first_term - second_term, mixed_term - first_term - second_term)


def by_columns(left_local, right_local, norm_scale):
    columns = lax.all_to_all(right_local, "idx", split_axis=1, concat_axis=2, tiled=True)
    merged = jnp.stack(
        complex_product(left_local[0], left_local[1], columns[0], columns[1], "bmk,bkn->bmn")
    )
    half_cols = merged.shape[3] // 2
    half_index = lax.axis_index("half")
    outgoing = lax.dynamic_slice_in_dim(merged, (1 - half_index) * half_cols, half_cols, 3)
    own_slab = lax.dynamic_slice_in_dim(merged, half_index * half_cols, half_cols, 3)
    other_slab = swapped(outgoing, "half", 0)
    is_lower = half_index == 0
    first_pair = jnp.where(is_lower, own_slab, other_slab)
    second_pair = jnp.where(is_lower, other_slab, own_slab)
    real_part, imag_part = complex_product(
        first_pair[0], first_pair[1], second_pair[0], second_pair[1], "bmn,bon->mo"
    )
    return jnp.stack([real_part, imag_part], axis=1) * norm_scale


def by_batch(left_local, right_local, norm_scale):
    idx, half = lax.axis_size("idx"), lax.axis_size("half")
    planes, batch, rows, between = right_local.shape
    mine = left_local.shape[1] // half
    half_index = lax.axis_index("half")
    blocks = right_local.reshape(planes, idx * half, mine, rows, between)
    sizes = CHUNKS if sum(CHUNKS) == mine else (mine,)
    received = []
    start = 0
    for size in sizes:
        piece = blocks[:, :, start:start + size].transpose(1, 0, 2, 3, 4)
        received.append(
            lax.all_to_all(piece, ("idx", "half"), split_axis=0, concat_axis=0, tiled=True)
        )
        start += size
    outgoing = lax.dynamic_slice_in_dim(left_local, (1 - half_index) * mine, mine, 1)
    own = lax.dynamic_slice_in_dim(left_local, half_index * mine, mine, 1)
    other = swapped(outgoing, "half", 0)
    is_lower = half_index == 0
    first = jnp.where(is_lower, own, other)
    second = jnp.where(is_lower, other, own)
    total = None
    start = 0
    for size, got in zip(sizes, received):
        got = got.reshape(idx, half, planes, size, rows, between)
        pairs = got.transpose(1, 2, 3, 0, 4, 5).reshape(half, planes, size, idx * rows, between)
        inner = complex_product(
            pairs[0, 0], pairs[0, 1], pairs[1, 0], pairs[1, 1], "bkn,bln->bkl"
        )
        a = first[:, start:start + size]
        b = second[:, start:start + size]
        partial = complex_product(a[0], a[1], inner[0], inner[1], "bmk,bkl->bml")
        term = complex_product(partial[0], partial[1], b[0], b[1], "bml,bol->mo")
        total = term if total is None else (total[0] + term[0], total[1] + term[1])
        start += size
    return jnp.stack(total, axis=1) * norm_scale


def on_device(left_factor, right_factor):
    left_local = left_factor[0]
    right_local = right_factor[0]
    batch, between = right_local.shape[1], right_local.shape[3]
    norm_scale = 1.0 / math.sqrt(2.0 * batch * between)
    shared = left_local.shape[1] % lax.axis_size("half") == 0
    form = by_batch if shared else by_columns
    return lax.psum_scatter(
        form(left_local, right_local, norm_scale),
        ("idx", "half"),
        scatter_dimension=0,
        tiled=True,
    )


def solution(mesh):
    return jax.shard_map(
        on_device,
        mesh=mesh,
        in_specs=(P("half", "cuts", "idx", None, None), P("half", "cuts", None, "idx", None)),
        out_specs=P(("idx", "half"), "cuts", None),
        check_vma=False,
    )
```
